32 devices in a mesh: groups: 1, slab: 8 (over z, y), temp: 2 (over x), pen: 2 (over core).
Axes of the slice: x: 2, y: 2, z: 4, core: 2. Of those that a mesh axis runs over, the one named last changes fastest.
Arguments:
- moments: float32 [2, 3, 128, 128, 128], P(('groups', 'temp'), None, ('slab', 'pen')), may hold values from -1 to 1, as said below
- couplings: bfloat16 [3, 128, 128, 128], P('groups', ('slab', 'pen')), may hold values from -6 to 6
- noise: bfloat16 [2, 2, 3, 128, 128, 128], P(None, ('groups', 'temp'), None, ('slab', 'pen')), may hold values from -6 to 6
- kernel: float32 [6, 128, 128, 128], P(None, None, ('slab', 'pen')), may hold values from -2.5 to 2.5, as said below
- temps: float32 [2], replicated, may hold values from 0.05 to 2
- order: int32 [2], P('groups'), may hold values from 0 to 1, each once
- accept: int32 [2], P('groups'), may hold values 0 or 1
Outputs:
- moments_out: float32 [2, 3, 128, 128, 128], P(('groups', 'temp'), None, ('slab', 'pen'))
- labels: int32 [2], P('groups')
The draws below stay inside these ranges and needn't reach their ends.
Inputs may be any that keep to these rules, and one draw needn't show every extreme that they name: `moments`: every moment vector (the three entries of one replica at one cell) has length one up to float32 rounding. kernel[c, i, j, l] equals kernel[c, (128 - i) % 128, (128 - j) % 128, (128 - l) % 128]. `order`: each temperature index appears once.
All inputs are finite; a program needn't handle non-finite values.
Results may differ from the reference program's by a relative error of at most 0.0003.
Values sent between devices are 32-bit elements; how exact they have to be, the bound alone decides.
A program may use at most 128 MiB of HBM per device.

```python
import math
import jax
import jax.numpy as jnp
from jax import lax

GRID = 128
STEPS = 2
REPL = 2


def draw_moments(key, part):
    shape = (REPL, GRID, GRID, GRID)
    key_height, key_phase = jax.random.split(jax.random.fold_in(key, 11))
    height = jax.random.uniform(key_height, shape, jnp.float32, -1.0, 1.0)
    phase = jax.random.uniform(key_phase, shape, jnp.float32, 0.0, 2.0 * math.pi)
    radial = jnp.sqrt(jnp.maximum(1.0 - height * height, 0.0))
    return jnp.stack([radial * jnp.cos(phase), radial * jnp.sin(phase), height], axis=1).astype(jnp.float32)


def draw_kernel(key, part):
    positions = jnp.arange(GRID, dtype=jnp.float32)
    wave = jnp.sin(2.0 * math.pi * positions / GRID)
    wave_x = wave[:, None, None]
    wave_y = wave[None, :, None]
    wave_z = wave[None, None, :]
    denominator = wave_x * wave_x + wave_y * wave_y + wave_z * wave_z + 0.05
    combos = [(wave_x, wave_x), (wave_y, wave_y), (wave_z, wave_z), (wave_x, wave_y), (wave_x, wave_z), (wave_y, wave_z)]
    physical = jnp.stack([left_wave * right_wave / denominator for left_wave, right_wave in combos])
    rough_key = jax.random.fold_in(key, 23)
    rough = jnp.clip(jax.random.normal(rough_key, (6, GRID, GRID, GRID), jnp.float32), -3.0, 3.0) * 0.4
    mirrored = jnp.roll(jnp.flip(rough, (1, 2, 3)), 1, axis=(1, 2, 3))
    return (0.8 * physical + 0.5 * (rough + mirrored)).astype(jnp.float32)


def plant(entries, key, least, top_value):
    longest = entries.shape.index(max(entries.shape))
    spots = []
    for shift in (0, 1):
        where = [jax.random.randint(jax.random.fold_in(key, axis), (), 0, length) for axis, length in enumerate(entries.shape)]
        where[longest] = (where[longest] + shift) % entries.shape[longest]
        spots.append(tuple(where))
    return entries.at[spots[0]].set(least).at[spots[1]].set(top_value)


def block_levels(rng, extent, cuts, low, high):
    factor_of, own = 1.0, jax.random.fold_in(rng, 6)
    for dim, blocks in cuts:
        draws = jnp.exp(jax.random.uniform(jax.random.fold_in(own, dim), (blocks,), jnp.float32, low / len(cuts), high / len(cuts)))
        factor_of = factor_of * jnp.repeat(draws, extent[dim] // blocks).reshape([-1 if axis == dim else 1 for axis in range(len(extent))])
    return factor_of


def scatter_about(rng, extent, width, most, pieces=(), held_as=jnp.bfloat16):
    factor_of = block_levels(rng, extent, pieces, -0.22, 0.18) if pieces else 1.0
    entries = jax.random.normal(rng, extent, jnp.float32) * width * factor_of
    return jnp.minimum(jnp.maximum(entries, -most), most).astype(held_as)


def setup_inputs(seed: int = 0, part: int = 0) -> dict:
    key_list = jax.random.split(jax.random.key(seed), 8)
    own_keys = jax.random.split(jax.random.fold_in(key_list[7], part), 8)
    moments = draw_moments(jax.random.fold_in(jax.random.fold_in(key_list[7], part), 71), part)
    couplings = scatter_about(own_keys[1], (3, GRID, GRID, GRID), 1.0, 6.0, ((1, 16),))
    noise = scatter_about(own_keys[2], (STEPS, REPL, 3, GRID, GRID, GRID), 1.0, 6.0, ((1, 2), (3, 16)))
    kernel = draw_kernel(jax.random.fold_in(key_list[7], 71), part)
    temps = jnp.clip(jnp.exp(jax.random.uniform(key_list[4], (REPL,), jnp.float32, math.log(0.05), math.log(2.0))), 0.05, 2.0)
    order = jax.random.permutation(own_keys[5], REPL).astype(jnp.int32)
    accept = plant((jax.random.randint(own_keys[6], (REPL,), 0, 4) < 3).astype(jnp.int32), jax.random.fold_in(own_keys[6], 1), 0, 1)
    return {"moments": moments, "couplings": couplings, "noise": noise, "kernel": kernel, "temps": temps, "order": order, "accept": accept}


TIME_STEP = 0.1
DAMPING = 0.5

def cross(left, right, axis):
    left_parts = [lax.index_in_dim(left, component, axis, keepdims=False) for component in range(3)]
    right_parts = [lax.index_in_dim(right, component, axis, keepdims=False) for component in range(3)]
    result = [left_parts[1] * right_parts[2] - left_parts[2] * right_parts[1], left_parts[2] * right_parts[0] - left_parts[0] * right_parts[2], left_parts[0] * right_parts[1] - left_parts[1] * right_parts[0]]
    return jnp.stack(result, axis=axis)

def pair_labels(order, accept):
    slot_index = jnp.arange(order.shape[0], dtype=jnp.int32)
    position = lax.optimization_barrier(jnp.sum(jnp.where(order[None, :] == slot_index[:, None], slot_index[None, :], 0), axis=1)).astype(jnp.int32)
    mate_position = position + 1 - 2 * (position % 2)
    partner = lax.optimization_barrier(jnp.sum(jnp.where(slot_index[None, :] == mate_position[:, None], order[None, :], 0), axis=1)).astype(jnp.int32)
    partner_flag = lax.optimization_barrier(jnp.sum(jnp.where(slot_index[None, :] == partner[:, None], accept[None, :], 0), axis=1)).astype(jnp.int32)
    accepted = accept * partner_flag
    return jnp.where(accepted == 1, partner, slot_index).astype(jnp.int32)

def slot_sigma(labels, temps):
    slot_index = jnp.arange(temps.shape[0], dtype=jnp.int32)
    picked = lax.optimization_barrier(jnp.sum(jnp.where(labels[:, None] == slot_index[None, :], temps[None, :], jnp.zeros_like(temps)[None, :]), axis=1))
    return jnp.sqrt(2.0 * DAMPING * picked / TIME_STEP)

def neighbor_sum(moment_field, bond_field):
    summed = jnp.zeros_like(moment_field)
    for grid_axis in range(3):
        coupling = bond_field[grid_axis]
        summed = summed + coupling * jnp.roll(moment_field, -1, grid_axis + 1) + jnp.roll(coupling * moment_field, 1, grid_axis + 1)
    return summed

def dipole(moment_field, kernel):
    spectrum = jnp.fft.fftn(moment_field, axes=(1, 2, 3))
    parts = [spectrum[0], spectrum[1], spectrum[2]]
    fields = [-(kernel[0] * parts[0] + kernel[3] * parts[1] + kernel[4] * parts[2]), -(kernel[3] * parts[0] + kernel[1] * parts[1] + kernel[5] * parts[2]), -(kernel[4] * parts[0] + kernel[5] * parts[1] + kernel[2] * parts[2])]
    return jnp.real(jnp.fft.ifftn(jnp.stack(fields), axes=(1, 2, 3)))

def advance(moment_field, local_field, noise_scale, noise_step):
    effective = local_field + noise_scale * noise_step.astype(jnp.float32)
    torque = cross(moment_field, effective, 0)
    stepped = moment_field - TIME_STEP * (torque + DAMPING * cross(moment_field, torque, 0))
    return stepped * lax.rsqrt(lax.optimization_barrier(jnp.sum(stepped * stepped, axis=0, keepdims=True)))

def reference(moments, couplings, noise, kernel, temps, order, accept):
    labels = pair_labels(order, accept)
    slot_index = jnp.arange(temps.shape[0], dtype=jnp.int32)
    first_scale = slot_sigma(slot_index, temps)
    second_scale = slot_sigma(labels, temps)
    bond_field = couplings.astype(jnp.float32)

    def one_replica(packed):
        moment_field, noises, scale_one, scale_two = packed
        for step_index, noise_scale in ((0, scale_one), (1, scale_two)):
            local_field = neighbor_sum(moment_field, bond_field) + dipole(moment_field, kernel)
            moment_field = advance(moment_field, local_field, noise_scale, noises[step_index])
        return moment_field
    moved = lax.map(one_replica, (moments, jnp.moveaxis(noise, 1, 0), first_scale, second_scale))
    return (moved, labels)
```

```python
import functools
import math

import jax
import jax.numpy as jnp
import numpy as np
from jax import lax
from jax.experimental import pallas as pl
from jax.experimental.pallas import tpu as pltpu
from jax.sharding import PartitionSpec as P

TIME_STEP = 0.1
DAMPING = 0.5
MESH = pl.DeviceIdType.MESH
F32 = jnp.float32
BF16 = jnp.bfloat16
PAIRS = ((0, 3, 4), (3, 1, 5), (4, 5, 2))


def trig(length):
    product = np.outer(np.arange(length), np.arange(length)) % length
    cosine = np.cos(2.0 * math.pi * product / length)
    sine = np.sin(2.0 * math.pi * product / length)
    sine[(2 * product) % length == 0] = 0.0
    return cosine, sine


def halves(table):
    table = table.astype(np.float32)
    high = table.astype(BF16)
    low = (table - high.astype(np.float32)).astype(BF16)
    return high, low


def left_table(table):
    high, low = halves(table)
    return np.concatenate([high, high, low], axis=1)


def right_table(table):
    high, low = halves(table)
    return np.concatenate([high, high, low], axis=0)


def split(values):
    high = values.astype(BF16)
    low = (values - high.astype(F32)).astype(BF16)
    return high, low


def dot_left(table, values):
    high, low = split(values)
    return jnp.dot(
        table, jnp.concatenate([high, low, high], axis=0), preferred_element_type=F32
    )


def dot_right(values, table):
    high, low = split(values)
    return jnp.dot(
        jnp.concatenate([high, low, high], axis=1), table, preferred_element_type=F32
    )


def build_tables(width, depth):
    cos_w, sin_w = trig(width)
    cos_d, sin_d = trig(depth)
    mid = depth // 2
    half = width // 2
    fwd_depth = np.concatenate([cos_d[:, :mid], -sin_d[:, :mid]], axis=1)
    fwd_depth[:, mid] = cos_d[:, mid]
    weight = np.where(np.arange(mid) == 0, 1.0, 2.0)[:, None]
    inv_depth = np.concatenate([weight * cos_d[:mid], -weight * sin_d[:mid]], axis=0)
    inv_depth[mid] = cos_d[mid]
    inv_depth = -inv_depth / depth
    fwd_width = np.concatenate([cos_w, sin_w], axis=0)
    inv_width = np.concatenate([cos_w, sin_w], axis=1) / width
    ky = np.arange(width)[:, None]
    lane = np.arange(depth)[None, :]
    lane0, lane_mid = lane == 0, lane == mid
    slot = lane0 | lane_mid
    low = (ky > 0) & (ky < half)
    high = ky > half
    edge = ~(low | high)
    sign = np.where(lane < mid, 1.0, -1.0)
    zero = np.zeros((width, depth))
    plain = zero + ~slot
    forward = [
        plain + (lane0 & ~high) + (lane_mid & edge),
        zero + (lane0 & high),
        plain * sign - (lane_mid & low),
        zero - (lane_mid & high),
    ]
    inverse = [
        plain + (slot & edge) + 2.0 * (lane0 & low),
        2.0 * (lane_mid & high),
        -plain * sign - 2.0 * (lane0 & low),
        -2.0 * (lane_mid & high),
    ]
    masks = np.stack(forward + inverse).astype(np.float32)
    return (
        right_table(fwd_depth),
        left_table(fwd_width),
        right_table(inv_depth),
        left_table(inv_width),
        masks,
    )


def make_kernel(slices, pens, planes, rows, width, depth):
    mid = depth // 2
    half = width // 2
    chunk = planes * rows
    per = 2
    parts = 2 if planes % (2 * per) == 0 and planes * rows % 16 == 0 else 1
    share = planes // parts
    layer = max(1, slices // 4)

    def turn(values):
        return pltpu.roll(values, mid, 1)

    def kernel(
        temps, order, accept, m_hbm, j_hbm, n_hbm, k_hbm,
        fwd_d_hbm, fwd_w_hbm, inv_d_hbm, inv_w_hbm, masks_hbm,
        out_hbm, labels, scales, fwd_d, fwd_w, inv_d, inv_w, masks,
        v, jj, nn, kk, kw, ks, spec, turned0, field, send_a, recv_a, send_b, recv_b,
        carry, above, below,
        load_sem, send_sem_a, recv_sem_a, send_sem_b, recv_sem_b, halo_send, halo_recv, out_sem,
    ):
        me = lax.axis_index("slab") * pens + lax.axis_index("pen")

        def place(index):
            return {"slab": index // pens, "pen": index % pens}

        loads = [
            pltpu.make_async_copy(source, target, load_sem.at[number])
            for number, (source, target) in enumerate(
                (
                    (fwd_d_hbm, fwd_d), (fwd_w_hbm, fwd_w),
                    (masks_hbm.at[pl.ds(0, 4)], masks.at[pl.ds(0, 4)]),
                    (m_hbm.at[0], v.at[0]), (m_hbm.at[1], v.at[1]), (m_hbm.at[2], v.at[2]),
                    (j_hbm, jj),
                    (inv_d_hbm, inv_d), (inv_w_hbm, inv_w),
                    (masks_hbm.at[pl.ds(4, 4)], masks.at[pl.ds(4, 4)]),
                    (k_hbm, kk), (n_hbm, nn),
                )
            )
        ]
        first_loads, early_loads, late_loads = loads[:4], loads[4:7], loads[7:]
        barrier = pltpu.get_barrier_semaphore()
        for load in first_loads:
            load.start()

        def greet(step, carried):
            pl.semaphore_signal(
                barrier, inc=1, device_id=place((me + step) % slices), device_id_type=MESH
            )
            return carried

        lax.fori_loop(1, slices, greet, 0)
        for load in early_loads + late_loads:
            load.start()

        count = temps.shape[0]
        replica = lax.axis_index("temp")

        def pick(source, index):
            chosen = source[0]
            for slot in range(1, count):
                chosen = jnp.where(index == slot, source[slot], chosen)
            return chosen

        names = list(range(count))
        for pair in range(count // 2):
            first, second = order[2 * pair], order[2 * pair + 1]
            both = pick(accept, first) * pick(accept, second) == 1
            for slot in range(count):
                names[slot] = jnp.where(
                    both & (first == slot),
                    second,
                    jnp.where(both & (second == slot), first, names[slot]),
                )
        swapped = jnp.int32(0)
        for slot in range(count):
            labels[slot] = names[slot]
            swapped = jnp.where(replica == slot, names[slot], swapped)
        for step, index in enumerate((replica, swapped)):
            heat = jnp.full((8, depth), 2.0 * DAMPING / TIME_STEP * pick(temps, index), F32)
            scales[step] = jnp.sqrt(heat)

        lane = lax.broadcasted_iota(jnp.int32, (width, depth), 1)
        next_one, last_one = (me + 1) % slices, (me + slices - 1) % slices

        def rows_of(index, pieces, piece):
            size = chunk // pieces
            return pl.ds(pl.multiple_of(index * chunk + piece * size, size), size)

        def exchange_copy(
            source, target, send_sem, recv_sem, pieces, component, piece, partner, origin
        ):
            return pltpu.make_async_remote_copy(
                src_ref=source.at[component, rows_of(partner, pieces, piece)],
                dst_ref=target.at[component, rows_of(origin, pieces, piece)],
                send_sem=send_sem.at[component, piece],
                recv_sem=recv_sem.at[component, piece],
                device_id=place(partner),
                device_id_type=MESH,
            )

        def own_copy(source, target, recv_sem, pieces, component, piece):
            return pltpu.make_async_copy(
                source.at[component, rows_of(me, pieces, piece)],
                target.at[component, rows_of(me, pieces, piece)],
                recv_sem.at[component, piece],
            )

        def is_near(partner):
            gap = partner // layer - me // layer
            return (gap >= -1) & (gap <= 1)

        def send_near(source, target, send_sem, recv_sem, pieces, component, piece):
            def one(step, carried):
                partner = (me + step) % slices

                @pl.when(is_near(partner))
                def _():
                    exchange_copy(
                        source, target, send_sem, recv_sem, pieces, component, piece, partner, me
                    ).start()

                return carried

            lax.fori_loop(1, slices, one, 0)
            own_copy(source, target, recv_sem, pieces, component, piece).start()

        def send_far(source, target, send_sem, recv_sem, pieces, component, piece):
            def one(step, carried):
                partner = (me + step) % slices

                @pl.when(jnp.logical_not(is_near(partner)))
                def _():
                    exchange_copy(
                        source, target, send_sem, recv_sem, pieces, component, piece, partner, me
                    ).start()

                return carried

            lax.fori_loop(1, slices, one, 0)

        def bulk(source, target, send_sem, recv_sem, pieces, component, piece, count):
            rows_moved = pl.ds(0, count * (chunk // pieces))
            return pltpu.make_async_remote_copy(
                src_ref=source.at[component, rows_moved],
                dst_ref=target.at[component, rows_moved],
                send_sem=send_sem.at[component, piece],
                recv_sem=recv_sem.at[component, piece],
                device_id=place(last_one),
                device_id_type=MESH,
            )

        def receive_all(*route):
            bulk(*route, slices).wait_recv()

        def sent_all(*route):
            bulk(*route, slices - 1).wait_send()

        route_a = (send_a, recv_a, send_sem_a, recv_sem_a, 1)
        route_b = (send_b, recv_b, send_sem_b, recv_sem_b, parts)

        up_copy = pltpu.make_async_remote_copy(
            src_ref=carry, dst_ref=below, send_sem=halo_send.at[0], recv_sem=halo_recv.at[0],
            device_id=place(next_one), device_id_type=MESH,
        )
        down_copy = pltpu.make_async_remote_copy(
            src_ref=v.at[:, 0], dst_ref=above, send_sem=halo_send.at[1],
            recv_sem=halo_recv.at[1], device_id=place(last_one), device_id_type=MESH,
        )

        def widen():
            for r in range(rows):
                ky = me * rows + r
                high = jnp.where(ky > half, 1, 0)
                edge = jnp.where((ky == 0) | (ky == half), 1, 0)
                low_lane = jnp.where(lane < mid, 1, 0)
                flip0 = jnp.where(lane == 0, high, 0)
                flip1 = jnp.where(lane == mid, high, 0)
                edge0 = jnp.where(lane == 0, edge, 0)
                edge1 = jnp.where(lane == mid, edge, 0)
                take = (low_lane + flip0 + flip1 + edge1) % 2 == 1
                take_sine = (low_lane + flip0 + flip1 + edge0) % 2 == 1
                for item in range(6):
                    plain = kk[item, pl.ds(r, width, stride=rows), :]
                    other = turn(plain)
                    wide = jnp.where(take, plain, other)
                    kw[item, r] = wide
                    if r == 0:
                        ks[item] = jnp.where(take_sine, plain, other) - wide

        def forward_compute(component, start=0, stop=planes):
            for first in range(start, stop, per):
                group = range(first, first + per)
                packed = [dot_right(v[component, x], fwd_d[...]) for x in group]
                both = dot_left(fwd_w[...], jnp.concatenate(packed, axis=1))
                for number, x in enumerate(group):
                    part = slice(number * depth, (number + 1) * depth)
                    cosine, sine = both[:width, part], both[width:, part]
                    result = (
                        cosine * masks[0]
                        + turn(cosine) * masks[1]
                        + turn(sine) * masks[2]
                        + sine * masks[3]
                    )
                    for target in range(slices):
                        row = target * chunk + x * rows
                        send_a[component, row : row + rows, :] = result[
                            target * rows : (target + 1) * rows
                        ]

        def forward_component(component, carried):
            forward_compute(component)
            send_near(*route_a, component, 0)
            return carried

        def neighbours(step):
            def one(component, carried):
                for x in range(planes):
                    here = v[component, x]
                    ahead = above[component] if x == planes - 1 else v[component, x + 1]
                    total = jj[0, x].astype(F32) * ahead
                    if x == 0:
                        total = total + below[component]
                    else:
                        total = total + jj[0, x - 1].astype(F32) * v[component, x - 1]
                    bond = jj[1, x].astype(F32)
                    total = total + bond * pltpu.roll(here, width - 1, 0)
                    total = total + pltpu.roll(bond * here, 1, 0)
                    bond = jj[2, x].astype(F32)
                    total = total + bond * pltpu.roll(here, depth - 1, 1)
                    total = total + pltpu.roll(bond * here, 1, 1)
                    field[component, x] = total + scales[step, 0:1, :] * nn[step, component, x].astype(F32)
                return carried

            lax.fori_loop(0, 3, one, 0)

        def cross_forward(component, carried):
            receive_all(*route_a, component, 0)
            sign = jnp.where(lane < mid, 1.0, -1.0)
            for first in range(0, rows, per):
                group = range(first, first + per)
                lines = [recv_a[component, pl.ds(r, width, stride=rows), :] for r in group]
                both = dot_left(fwd_w[...], jnp.concatenate(lines, axis=1))
                for number, r in enumerate(group):
                    part = slice(number * depth, (number + 1) * depth)
                    cosine, sine = both[:width, part], both[width:, part]
                    sine = turn(sine) * sign
                    spec[component, r] = cosine + sine
                    if r == 0:
                        turned0[component] = sine
            return carried

        def cross_inverse(component):
            sign = jnp.where(lane < mid, -1.0, 1.0)
            items = PAIRS[component]
            for first in range(0, rows, per):
                group = range(first, first + per)
                plain, quarter = [], []
                for r in group:
                    value = (
                        kw[items[0], r] * spec[0, r]
                        + kw[items[1], r] * spec[1, r]
                        + kw[items[2], r] * spec[2, r]
                    )
                    if r == 0:
                        value = value + (
                            ks[items[0]] * turned0[0]
                            + ks[items[1]] * turned0[1]
                            + ks[items[2]] * turned0[2]
                        )
                    plain.append(value)
                    quarter.append(turn(value) * sign)
                stacked = jnp.concatenate(
                    [jnp.concatenate(plain, axis=1), jnp.concatenate(quarter, axis=1)], axis=0
                )
                result = dot_left(inv_w[...], stacked)
                for number, r in enumerate(group):
                    send_b[component, pl.ds(r, width, stride=rows), :] = result[
                        :, number * depth : (number + 1) * depth
                    ]
            for piece in range(parts):
                send_near(*route_b, component, piece)

        def inverse_component(piece, component, carried):
            receive_all(*route_b, component, piece)
            for first in range(piece * share, (piece + 1) * share, per):
                group = range(first, first + per)
                plain, quarter = [], []
                for x in group:
                    value = jnp.concatenate(
                        [
                            recv_b[component, s * chunk + x * rows : s * chunk + (x + 1) * rows, :]
                            for s in range(slices)
                        ],
                        axis=0,
                    )
                    other = turn(value)
                    plain.append(value * masks[4] + other * masks[5])
                    quarter.append(other * masks[6] + value * masks[7])
                stacked = jnp.concatenate(
                    [jnp.concatenate(plain, axis=1), jnp.concatenate(quarter, axis=1)], axis=0
                )
                result = dot_left(inv_w[...], stacked)
                for number, x in enumerate(group):
                    field[component, x] += dot_right(
                        result[:, number * depth : (number + 1) * depth], inv_d[...]
                    )
            return carried

        def advance(x, carried):
            block = math.gcd(width, 32)
            for start in range(0, width, block):
                part = slice(start, start + block)
                m = [v[c, x, part] for c in range(3)]
                h = [field[c, x, part] for c in range(3)]

                def product(a, b):
                    return [
                        a[1] * b[2] - a[2] * b[1],
                        a[2] * b[0] - a[0] * b[2],
                        a[0] * b[1] - a[1] * b[0],
                    ]

                t = product(m, h)
                w = product(m, t)
                u = [m[c] - TIME_STEP * (t[c] + DAMPING * w[c]) for c in range(3)]
                scale = lax.rsqrt(u[0] * u[0] + u[1] * u[1] + u[2] * u[2])
                for c in range(3):
                    v[c, x, part] = u[c] * scale
            return carried

        out_copies = [
            pltpu.make_async_copy(
                v.at[:, pl.ds(piece * share, share)],
                out_hbm.at[:, pl.ds(piece * share, share)],
                out_sem.at[piece],
            )
            for piece in range(parts)
        ]

        for load in first_loads:
            load.wait()
        forward_compute(0)
        for load in early_loads:
            load.wait()
        pl.semaphore_wait(barrier, slices - 1)

        def step_body(step, carried):
            send_near(*route_a, 0, 0)
            for c in range(3):
                carry[c] = jj[0, planes - 1].astype(F32) * v[c, planes - 1]
            down_copy.start()
            up_copy.start()
            lax.fori_loop(1, 3, forward_component, 0)
            for c in range(3):
                send_far(*route_a, c, 0)

            @pl.when(step == 0)
            def _():
                for load in late_loads:
                    load.wait()
                widen()

            up_copy.wait()
            down_copy.wait()
            neighbours(step)
            lax.fori_loop(0, 3, cross_forward, 0)
            for c in range(3):
                cross_inverse(c)
            for piece in range(parts):
                for c in range(3):
                    send_far(*route_b, c, piece)
            for c in range(3):
                sent_all(*route_a, c, 0)
            for piece in range(parts):
                lax.fori_loop(0, 3, functools.partial(inverse_component, piece), 0)
                lax.fori_loop(piece * share, (piece + 1) * share, advance, 0)

                @pl.when(step == 0)
                def _():
                    forward_compute(0, piece * share, (piece + 1) * share)

                @pl.when(step == 1)
                def _():
                    out_copies[piece].start()

            for piece in range(parts):
                for c in range(3):
                    sent_all(*route_b, c, piece)
            return carried

        lax.fori_loop(0, 2, step_body, 0)
        for copy in out_copies:
            copy.wait()

    return kernel


def on_device(moments, couplings, noise, kernel, temps, order, accept):
    planes, width, depth = moments.shape[2:]
    pens = lax.axis_size("pen")
    slices = lax.axis_size("slab") * pens
    rows = width // slices
    tables = [jnp.asarray(table) for table in build_tables(width, depth)]
    any_spec = pl.BlockSpec(memory_space=pl.ANY)
    cells = (3, planes, width, depth)
    flat = (3, width * rows, depth)
    dma = pltpu.SemaphoreType.DMA
    smem = pl.BlockSpec(memory_space=pltpu.SMEM)
    moved, labels = pl.pallas_call(
        make_kernel(slices, pens, planes, rows, width, depth),
        out_shape=(
            jax.ShapeDtypeStruct(cells, F32),
            jax.ShapeDtypeStruct(order.shape, jnp.int32),
        ),
        in_specs=[smem] * 3 + [any_spec] * 9,
        out_specs=(any_spec, smem),
        scratch_shapes=[
            pltpu.VMEM((2, 8, depth), F32),
        ] + [pltpu.VMEM(table.shape, table.dtype) for table in tables] + [
            pltpu.VMEM(cells, F32),
            pltpu.VMEM(cells, BF16),
            pltpu.VMEM((2,) + cells, BF16),
            pltpu.VMEM((6, width * rows, depth), F32),
            pltpu.VMEM((6, rows, width, depth), F32),
            pltpu.VMEM((6, width, depth), F32),
            pltpu.VMEM((3, rows, width, depth), F32),
            pltpu.VMEM((3, width, depth), F32),
            pltpu.VMEM(cells, F32),
            pltpu.VMEM(flat, F32),
            pltpu.VMEM(flat, F32),
            pltpu.VMEM(flat, F32),
            pltpu.VMEM(flat, F32),
            pltpu.VMEM((3, width, depth), F32),
            pltpu.VMEM((3, width, depth), F32),
            pltpu.VMEM((3, width, depth), F32),
            dma((12,)),
            dma((3, 1)),
            dma((3, 1)),
            dma((3, 2)),
            dma((3, 2)),
            dma((2,)),
            dma((2,)),
            dma((2,)),
        ],
        compiler_params=pltpu.CompilerParams(
            collective_id=0, has_side_effects=True, vmem_limit_bytes=60 * 1024 * 1024
        ),
        name="langevin",
    )(
        temps,
        order,
        accept,
        moments.reshape(cells),
        couplings,
        noise.reshape((2,) + cells),
        kernel.reshape(6, width * rows, depth),
        *tables,
    )
    return (moved.reshape(moments.shape), labels)


def solution(mesh):
    return jax.shard_map(
        on_device,
        mesh=mesh,
        in_specs=(
            P(("groups", "temp"), None, ("slab", "pen"), None, None),
            P("groups", ("slab", "pen"), None, None),
            P(None, ("groups", "temp"), None, ("slab", "pen"), None, None),
            P(None, None, ("slab", "pen"), None),
            P(),
            P("groups"),
            P("groups"),
        ),
        out_specs=(P(("groups", "temp"), None, ("slab", "pen"), None, None), P("groups")),
        check_vma=False,
    )
```

```python
import functools
import math

import jax
import jax.numpy as jnp
import numpy as np
from jax import lax
from jax.experimental import pallas as pl
from jax.experimental.pallas import tpu as pltpu
from jax.sharding import PartitionSpec as P

TIME_STEP = 0.1
DAMPING = 0.5
MESH = pl.DeviceIdType.MESH
F32 = jnp.float32
BF16 = jnp.bfloat16
PAIRS = ((0, 3, 4), (3, 1, 5), (4, 5, 2))


def trig(length):
    product = np.outer(np.arange(length), np.arange(length)) % length
    cosine = np.cos(2.0 * math.pi * product / length)
    sine = np.sin(2.0 * math.pi * product / length)
    sine[(2 * product) % length == 0] = 0.0
    return cosine, sine


def halves(table):
    table = table.astype(np.float32)
    high = table.astype(BF16)
    low = (table - high.astype(np.float32)).astype(BF16)
    return high, low


def left_table(table):
    high, low = halves(table)
    return np.concatenate([high, high, low], axis=1)


def right_table(table):
    high, low = halves(table)
    return np.concatenate([high, high, low], axis=0)


def split(values):
    high = values.astype(BF16)
    low = (values - high.astype(F32)).astype(BF16)
    return high, low


def dot_left(table, values):
    high, low = split(values)
    return jnp.dot(
        table, jnp.concatenate([high, low, high], axis=0), preferred_element_type=F32
    )


def dot_right(values, table):
    high, low = split(values)
    return jnp.dot(
        jnp.concatenate([high, low, high], axis=1), table, preferred_element_type=F32
    )


def build_tables(width, depth):
    cos_w, sin_w = trig(width)
    cos_d, sin_d = trig(depth)
    mid = depth // 2
    half = width // 2
    fwd_depth = np.concatenate([cos_d[:, :mid], -sin_d[:, :mid]], axis=1)
    fwd_depth[:, mid] = cos_d[:, mid]
    weight = np.where(np.arange(mid) == 0, 1.0, 2.0)[:, None]
    inv_depth = np.concatenate([weight * cos_d[:mid], -weight * sin_d[:mid]], axis=0)
    inv_depth[mid] = cos_d[mid]
    inv_depth = -inv_depth / depth
    fwd_width = np.concatenate([cos_w, sin_w], axis=0)
    inv_width = np.concatenate([cos_w, sin_w], axis=1) / width
    ky = np.arange(width)[:, None]
    lane = np.arange(depth)[None, :]
    lane0, lane_mid = lane == 0, lane == mid
    slot = lane0 | lane_mid
    low = (ky > 0) & (ky < half)
    high = ky > half
    edge = ~(low | high)
    sign = np.where(lane < mid, 1.0, -1.0)
    zero = np.zeros((width, depth))
    plain = zero + ~slot
    forward = [
        plain + (lane0 & ~high) + (lane_mid & edge),
        zero + (lane0 & high),
        plain * sign - (lane_mid & low),
        zero - (lane_mid & high),
    ]
    inverse = [
        plain + (slot & edge) + 2.0 * (lane0 & low),
        2.0 * (lane_mid & high),
        -plain * sign - 2.0 * (lane0 & low),
        -2.0 * (lane_mid & high),
    ]
    masks = np.stack(forward + inverse).astype(np.float32)
    return (
        right_table(fwd_depth),
        left_table(fwd_width),
        right_table(inv_depth),
        left_table(inv_width),
        masks,
    )


def make_kernel(slices, pens, planes, rows, width, depth):
    mid = depth // 2
    half = width // 2
    chunk = planes * rows
    per = 2
    parts = 2 if planes % (2 * per) == 0 and planes * rows % 16 == 0 else 1
    share = planes // parts
    layer = max(1, slices // 4)

    def turn(values):
        return pltpu.roll(values, mid, 1)

    def kernel(
        temps, order, accept, m_hbm, j_hbm, n_hbm, k_hbm,
        fwd_d_hbm, fwd_w_hbm, inv_d_hbm, inv_w_hbm, masks_hbm,
        out, labels, scales, fwd_d, fwd_w, inv_d, inv_w, masks,
        v, jj, nn, kk, kw, ks, spec, turned0, field, send_a, recv_a, send_b, recv_b,
        carry, above, below,
        load_sem, send_sem_a, recv_sem_a, send_sem_b, recv_sem_b, halo_send, halo_recv,
    ):
        me = lax.axis_index("slab") * pens + lax.axis_index("pen")

        def place(index):
            return {"slab": index // pens, "pen": index % pens}

        loads = [
            pltpu.make_async_copy(source, target, load_sem.at[number])
            for number, (source, target) in enumerate(
                (
                    (fwd_d_hbm, fwd_d), (fwd_w_hbm, fwd_w),
                    (masks_hbm.at[pl.ds(0, 4)], masks.at[pl.ds(0, 4)]),
                    (m_hbm.at[0], v.at[0]), (m_hbm.at[1], v.at[1]), (m_hbm.at[2], v.at[2]),
                    (j_hbm, jj),
                    (inv_d_hbm, inv_d), (inv_w_hbm, inv_w),
                    (masks_hbm.at[pl.ds(4, 4)], masks.at[pl.ds(4, 4)]),
                    (k_hbm, kk), (n_hbm, nn),
                )
            )
        ]
        first_loads, early_loads, late_loads = loads[:4], loads[4:7], loads[7:]
        barrier = pltpu.get_barrier_semaphore()
        for load in first_loads:
            load.start()

        def greet(step, carried):
            pl.semaphore_signal(
                barrier, inc=1, device_id=place((me + step) % slices), device_id_type=MESH
            )
            return carried

        lax.fori_loop(1, slices, greet, 0)
        for load in early_loads + late_loads:
            load.start()

        count = temps.shape[0]
        replica = lax.axis_index("temp")

        def pick(source, index):
            chosen = source[0]
            for slot in range(1, count):
                chosen = jnp.where(index == slot, source[slot], chosen)
            return chosen

        names = list(range(count))
        for pair in range(count // 2):
            first, second = order[2 * pair], order[2 * pair + 1]
            both = pick(accept, first) * pick(accept, second) == 1
            for slot in range(count):
                names[slot] = jnp.where(
                    both & (first == slot),
                    second,
                    jnp.where(both & (second == slot), first, names[slot]),
                )
        swapped = jnp.int32(0)
        for slot in range(count):
            labels[slot] = names[slot]
            swapped = jnp.where(replica == slot, names[slot], swapped)
        for step, index in enumerate((replica, swapped)):
            heat = jnp.full((8, depth), 2.0 * DAMPING / TIME_STEP * pick(temps, index), F32)
            scales[step] = jnp.sqrt(heat)

        lane = lax.broadcasted_iota(jnp.int32, (width, depth), 1)
        next_one, last_one = (me + 1) % slices, (me + slices - 1) % slices

        def rows_of(index, pieces, piece):
            size = chunk // pieces
            return pl.ds(pl.multiple_of(index * chunk + piece * size, size), size)

        def exchange_copy(
            source, target, send_sem, recv_sem, pieces, component, piece, partner, origin
        ):
            return pltpu.make_async_remote_copy(
                src_ref=source.at[component, rows_of(partner, pieces, piece)],
                dst_ref=target.at[component, rows_of(origin, pieces, piece)],
                send_sem=send_sem.at[component, piece],
                recv_sem=recv_sem.at[component, piece],
                device_id=place(partner),
                device_id_type=MESH,
            )

        def own_copy(source, target, recv_sem, pieces, component, piece):
            return pltpu.make_async_copy(
                source.at[component, rows_of(me, pieces, piece)],
                target.at[component, rows_of(me, pieces, piece)],
                recv_sem.at[component, piece],
            )

        def send_gaps(low, high, source, target, send_sem, recv_sem, pieces, component, piece):
            def one(step, carried):
                partner = (me + step) % slices
                gap = jnp.abs(partner // layer - me // layer)

                @pl.when((gap >= low) & (gap <= high))
                def _():
                    exchange_copy(
                        source, target, send_sem, recv_sem, pieces, component, piece, partner, me
                    ).start()

                return carried

            lax.fori_loop(1, slices, one, 0)

        def send_near(source, target, send_sem, recv_sem, pieces, component, piece):
            send_gaps(0, 1, source, target, send_sem, recv_sem, pieces, component, piece)
            own_copy(source, target, recv_sem, pieces, component, piece).start()

        def bulk(source, target, send_sem, recv_sem, pieces, component, piece, count):
            rows_moved = pl.ds(0, count * (chunk // pieces))
            return pltpu.make_async_remote_copy(
                src_ref=source.at[component, rows_moved],
                dst_ref=target.at[component, rows_moved],
                send_sem=send_sem.at[component, piece],
                recv_sem=recv_sem.at[component, piece],
                device_id=place(last_one),
                device_id_type=MESH,
            )

        def receive_all(*route):
            bulk(*route, slices).wait_recv()

        def sent_all(*route):
            bulk(*route, slices - 1).wait_send()

        route_a = (send_a, recv_a, send_sem_a, recv_sem_a, 1)
        route_b = (send_b, recv_b, send_sem_b, recv_sem_b, parts)

        up_copy = pltpu.make_async_remote_copy(
            src_ref=carry, dst_ref=below, send_sem=halo_send.at[0], recv_sem=halo_recv.at[0],
            device_id=place(next_one), device_id_type=MESH,
        )
        down_copy = pltpu.make_async_remote_copy(
            src_ref=v.at[:, 0], dst_ref=above, send_sem=halo_send.at[1],
            recv_sem=halo_recv.at[1], device_id=place(last_one), device_id_type=MESH,
        )

        def widen():
            for r in range(rows):
                ky = me * rows + r
                high = jnp.where(ky > half, 1, 0)
                edge = jnp.where((ky == 0) | (ky == half), 1, 0)
                low_lane = jnp.where(lane < mid, 1, 0)
                flip0 = jnp.where(lane == 0, high, 0)
                flip1 = jnp.where(lane == mid, high, 0)
                edge0 = jnp.where(lane == 0, edge, 0)
                edge1 = jnp.where(lane == mid, edge, 0)
                take = (low_lane + flip0 + flip1 + edge1) % 2 == 1
                take_sine = (low_lane + flip0 + flip1 + edge0) % 2 == 1
                for item in range(6):
                    plain = kk[item, pl.ds(r, width, stride=rows), :]
                    other = turn(plain)
                    wide = jnp.where(take, plain, other)
                    kw[item, r] = wide
                    if r == 0:
                        ks[item] = jnp.where(take_sine, plain, other) - wide

        def forward_compute(component, start=0, stop=planes):
            for first in range(start, stop, per):
                group = range(first, first + per)
                packed = [dot_right(v[component, x], fwd_d[...]) for x in group]
                both = dot_left(fwd_w[...], jnp.concatenate(packed, axis=1))
                for number, x in enumerate(group):
                    part = slice(number * depth, (number + 1) * depth)
                    cosine, sine = both[:width, part], both[width:, part]
                    result = (
                        cosine * masks[0]
                        + turn(cosine) * masks[1]
                        + turn(sine) * masks[2]
                        + sine * masks[3]
                    )
                    for target in range(slices):
                        row = target * chunk + x * rows
                        send_a[component, row : row + rows, :] = result[
                            target * rows : (target + 1) * rows
                        ]

        def forward_component(component, carried):
            forward_compute(component)
            send_near(*route_a, component, 0)
            return carried

        def neighbours(step):
            def one(component, carried):
                for x in range(planes):
                    here = v[component, x]
                    ahead = above[component] if x == planes - 1 else v[component, x + 1]
                    total = jj[0, x].astype(F32) * ahead
                    if x == 0:
                        total = total + below[component]
                    else:
                        total = total + jj[0, x - 1].astype(F32) * v[component, x - 1]
                    bond = jj[1, x].astype(F32)
                    total = total + bond * pltpu.roll(here, width - 1, 0)
                    total = total + pltpu.roll(bond * here, 1, 0)
                    bond = jj[2, x].astype(F32)
                    total = total + bond * pltpu.roll(here, depth - 1, 1)
                    total = total + pltpu.roll(bond * here, 1, 1)
                    field[component, x] = total + scales[step, 0:1, :] * nn[step, component, x].astype(F32)
                return carried

            lax.fori_loop(0, 3, one, 0)

        def cross_forward(component, carried):
            receive_all(*route_a, component, 0)
            sign = jnp.where(lane < mid, 1.0, -1.0)
            for first in range(0, rows, per):
                group = range(first, first + per)
                lines = [recv_a[component, pl.ds(r, width, stride=rows), :] for r in group]
                both = dot_left(fwd_w[...], jnp.concatenate(lines, axis=1))
                for number, r in enumerate(group):
                    part = slice(number * depth, (number + 1) * depth)
                    cosine, sine = both[:width, part], both[width:, part]
                    sine = turn(sine) * sign
                    spec[component, r] = cosine + sine
                    if r == 0:
                        turned0[component] = sine
            return carried

        def cross_inverse(component):
            sign = jnp.where(lane < mid, -1.0, 1.0)
            items = PAIRS[component]
            for first in range(0, rows, per):
                group = range(first, first + per)
                plain, quarter = [], []
                for r in group:
                    value = (
                        kw[items[0], r] * spec[0, r]
                        + kw[items[1], r] * spec[1, r]
                        + kw[items[2], r] * spec[2, r]
                    )
                    if r == 0:
                        value = value + (
                            ks[items[0]] * turned0[0]
                            + ks[items[1]] * turned0[1]
                            + ks[items[2]] * turned0[2]
                        )
                    plain.append(value)
                    quarter.append(turn(value) * sign)
                stacked = jnp.concatenate(
                    [jnp.concatenate(plain, axis=1), jnp.concatenate(quarter, axis=1)], axis=0
                )
                result = dot_left(inv_w[...], stacked)
                for number, r in enumerate(group):
                    send_b[component, pl.ds(r, width, stride=rows), :] = result[
                        :, number * depth : (number + 1) * depth
                    ]
            for piece in range(parts):
                send_near(*route_b, component, piece)

        def inverse_component(piece, component, carried):
            receive_all(*route_b, component, piece)
            for first in range(piece * share, (piece + 1) * share, per):
                group = range(first, first + per)
                plain, quarter = [], []
                for x in group:
                    value = jnp.concatenate(
                        [
                            recv_b[component, s * chunk + x * rows : s * chunk + (x + 1) * rows, :]
                            for s in range(slices)
                        ],
                        axis=0,
                    )
                    other = turn(value)
                    plain.append(value * masks[4] + other * masks[5])
                    quarter.append(other * masks[6] + value * masks[7])
                stacked = jnp.concatenate(
                    [jnp.concatenate(plain, axis=1), jnp.concatenate(quarter, axis=1)], axis=0
                )
                result = dot_left(inv_w[...], stacked)
                for number, x in enumerate(group):
                    field[component, x] += dot_right(
                        result[:, number * depth : (number + 1) * depth], inv_d[...]
                    )
            return carried

        def advance(x, carried):
            block = math.gcd(width, 32)
            for start in range(0, width, block):
                part = slice(start, start + block)
                m = [v[c, x, part] for c in range(3)]
                h = [field[c, x, part] for c in range(3)]

                def product(a, b):
                    return [
                        a[1] * b[2] - a[2] * b[1],
                        a[2] * b[0] - a[0] * b[2],
                        a[0] * b[1] - a[1] * b[0],
                    ]

                t = product(m, h)
                w = product(m, t)
                u = [m[c] - TIME_STEP * (t[c] + DAMPING * w[c]) for c in range(3)]
                scale = lax.rsqrt(u[0] * u[0] + u[1] * u[1] + u[2] * u[2])
                for c in range(3):
                    moved = u[c] * scale
                    v[c, x, part] = moved
                    out[c, x, part] = moved
            return carried

        for load in first_loads:
            load.wait()
        forward_compute(0)
        for load in early_loads:
            load.wait()
        pl.semaphore_wait(barrier, slices - 1)

        def step_body(step, carried):
            send_near(*route_a, 0, 0)
            for c in range(3):
                carry[c] = jj[0, planes - 1].astype(F32) * v[c, planes - 1]
            down_copy.start()
            up_copy.start()
            lax.fori_loop(1, 3, forward_component, 0)
            for c in range(3):
                send_gaps(2, 2, *route_a, c, 0)
            for c in range(3):
                send_gaps(3, 3, *route_a, c, 0)

            @pl.when(step == 0)
            def _():
                for load in late_loads:
                    load.wait()
                widen()

            up_copy.wait()
            down_copy.wait()
            neighbours(step)
            lax.fori_loop(0, 3, cross_forward, 0)
            for c in range(3):
                cross_inverse(c)
            for piece in range(parts):
                for c in range(3):
                    send_gaps(2, 2, *route_b, c, piece)
                for c in range(3):
                    send_gaps(3, 3, *route_b, c, piece)
            for c in range(3):
                sent_all(*route_a, c, 0)
            for piece in range(parts):
                lax.fori_loop(0, 3, functools.partial(inverse_component, piece), 0)
                lax.fori_loop(piece * share, (piece + 1) * share, advance, 0)

                @pl.when(step == 0)
                def _():
                    forward_compute(0, piece * share, (piece + 1) * share)

            for piece in range(parts):
                for c in range(3):
                    sent_all(*route_b, c, piece)
            return carried

        lax.fori_loop(0, 2, step_body, 0)

    return kernel


def on_device(moments, couplings, noise, kernel, temps, order, accept):
    planes, width, depth = moments.shape[2:]
    pens = lax.axis_size("pen")
    slices = lax.axis_size("slab") * pens
    rows = width // slices
    tables = [jnp.asarray(table) for table in build_tables(width, depth)]
    any_spec = pl.BlockSpec(memory_space=pl.ANY)
    cells = (3, planes, width, depth)
    flat = (3, width * rows, depth)
    dma = pltpu.SemaphoreType.DMA
    smem = pl.BlockSpec(memory_space=pltpu.SMEM)
    moved, labels = pl.pallas_call(
        make_kernel(slices, pens, planes, rows, width, depth),
        out_shape=(
            pltpu.VMEM(cells, F32),
            jax.ShapeDtypeStruct(order.shape, jnp.int32),
        ),
        in_specs=[smem] * 3 + [any_spec] * 9,
        out_specs=(pl.BlockSpec(memory_space=pltpu.VMEM), smem),
        scratch_shapes=[
            pltpu.VMEM((2, 8, depth), F32),
        ] + [pltpu.VMEM(table.shape, table.dtype) for table in tables] + [
            pltpu.VMEM(cells, F32),
            pltpu.VMEM(cells, BF16),
            pltpu.VMEM((2,) + cells, BF16),
            pltpu.VMEM((6, width * rows, depth), F32),
            pltpu.VMEM((6, rows, width, depth), F32),
            pltpu.VMEM((6, width, depth), F32),
            pltpu.VMEM((3, rows, width, depth), F32),
            pltpu.VMEM((3, width, depth), F32),
            pltpu.VMEM(cells, F32),
            pltpu.VMEM(flat, F32),
            pltpu.VMEM(flat, F32),
            pltpu.VMEM(flat, F32),
            pltpu.VMEM(flat, F32),
            pltpu.VMEM((3, width, depth), F32),
            pltpu.VMEM((3, width, depth), F32),
            pltpu.VMEM((3, width, depth), F32),
            dma((12,)),
            dma((3, 1)),
            dma((3, 1)),
            dma((3, 2)),
            dma((3, 2)),
            dma((2,)),
            dma((2,)),
        ],
        compiler_params=pltpu.CompilerParams(
            collective_id=0, has_side_effects=True, vmem_limit_bytes=60 * 1024 * 1024
        ),
        name="langevin",
    )(
        temps,
        order,
        accept,
        moments.reshape(cells),
        couplings,
        noise.reshape((2,) + cells),
        kernel.reshape(6, width * rows, depth),
        *tables,
    )
    return (moved.reshape(moments.shape), labels)


def solution(mesh):
    return jax.shard_map(
        on_device,
        mesh=mesh,
        in_specs=(
            P(("groups", "temp"), None, ("slab", "pen"), None, None),
            P("groups", ("slab", "pen"), None, None),
            P(None, ("groups", "temp"), None, ("slab", "pen"), None, None),
            P(None, None, ("slab", "pen"), None),
            P(),
            P("groups"),
            P("groups"),
        ),
        out_specs=(P(("groups", "temp"), None, ("slab", "pen"), None, None), P("groups")),
        check_vma=False,
    )
```

```python
import functools
import math

import jax
import jax.numpy as jnp
import numpy as np
from jax import lax
from jax.experimental import pallas as pl
from jax.experimental.pallas import tpu as pltpu
from jax.sharding import PartitionSpec as P

TIME_STEP = 0.1
DAMPING = 0.5
MESH = pl.DeviceIdType.MESH
F32 = jnp.float32
BF16 = jnp.bfloat16
PAIRS = ((0, 3, 4), (3, 1, 5), (4, 5, 2))


def trig(length):
    product = np.outer(np.arange(length), np.arange(length)) % length
    cosine = np.cos(2.0 * math.pi * product / length)
    sine = np.sin(2.0 * math.pi * product / length)
    sine[(2 * product) % length == 0] = 0.0
    return cosine, sine


def halves(table):
    table = table.astype(np.float32)
    high = table.astype(BF16)
    low = (table - high.astype(np.float32)).astype(BF16)
    return high, low


def left_table(table):
    high, low = halves(table)
    return np.concatenate([high, high, low], axis=1)


def right_table(table):
    high, low = halves(table)
    return np.concatenate([high, high, low], axis=0)


def split(values):
    high = values.astype(BF16)
    low = (values - high.astype(F32)).astype(BF16)
    return high, low


def dot_left(table, values):
    high, low = split(values)
    return jnp.dot(
        table, jnp.concatenate([high, low, high], axis=0), preferred_element_type=F32
    )


def dot_right(values, table):
    high, low = split(values)
    return jnp.dot(
        jnp.concatenate([high, low, high], axis=1), table, preferred_element_type=F32
    )


def build_tables(width, depth):
    cos_w, sin_w = trig(width)
    cos_d, sin_d = trig(depth)
    mid = depth // 2
    half = width // 2
    fwd_depth = np.concatenate([cos_d[:, :mid], -sin_d[:, :mid]], axis=1)
    fwd_depth[:, mid] = cos_d[:, mid]
    weight = np.where(np.arange(mid) == 0, 1.0, 2.0)[:, None]
    inv_depth = np.concatenate([weight * cos_d[:mid], -weight * sin_d[:mid]], axis=0)
    inv_depth[mid] = cos_d[mid]
    inv_depth = -inv_depth / depth
    fwd_width = np.concatenate([cos_w, sin_w], axis=0)
    inv_width = np.concatenate([cos_w, sin_w], axis=1) / width
    ky = np.arange(width)[:, None]
    lane = np.arange(depth)[None, :]
    lane0, lane_mid = lane == 0, lane == mid
    slot = lane0 | lane_mid
    low = (ky > 0) & (ky < half)
    high = ky > half
    edge = ~(low | high)
    sign = np.where(lane < mid, 1.0, -1.0)
    zero = np.zeros((width, depth))
    plain = zero + ~slot
    forward = [
        plain + (lane0 & ~high) + (lane_mid & edge),
        zero + (lane0 & high),
        plain * sign - (lane_mid & low),
        zero - (lane_mid & high),
    ]
    inverse = [
        plain + (slot & edge) + 2.0 * (lane0 & low),
        2.0 * (lane_mid & high),
        -plain * sign - 2.0 * (lane0 & low),
        -2.0 * (lane_mid & high),
    ]
    masks = np.stack(forward + inverse).astype(np.float32)
    return (
        right_table(fwd_depth),
        left_table(fwd_width),
        right_table(inv_depth),
        left_table(inv_width),
        masks,
    )


def make_kernel(slices, pens, planes, rows, width, depth):
    mid = depth // 2
    half = width // 2
    chunk = planes * rows
    per = 2
    parts = 2 if planes % (2 * per) == 0 and planes * rows % 16 == 0 else 1
    share = planes // parts
    layer = max(1, slices // 4)
    layers = slices // layer

    def turn(values):
        return pltpu.roll(values, mid, 1)

    def kernel(
        temps_hbm, order_hbm, accept_hbm, m_hbm, j_hbm, n_hbm, k_hbm,
        fwd_d_hbm, fwd_w_hbm, inv_d_hbm, inv_w_hbm, masks_hbm,
        out, labels, temps, order, accept, scales, fwd_d, fwd_w, inv_d, inv_w, masks,
        v, jj, nn, kk, kw, ks, spec, turned0, field, send_a, recv_a, send_b, recv_b,
        carry, above, below,
        load_sem, send_sem_a, recv_sem_a, send_sem_b, recv_sem_b, halo_send, halo_recv,
    ):
        me = lax.axis_index("slab") * pens + lax.axis_index("pen")

        def place(index):
            return {"slab": lax.div(index, pens), "pen": lax.rem(index, pens)}

        loads = [
            pltpu.make_async_copy(source, target, load_sem.at[number])
            for number, (source, target) in enumerate(
                (
                    (fwd_d_hbm, fwd_d), (fwd_w_hbm, fwd_w),
                    (masks_hbm.at[pl.ds(0, 4)], masks.at[pl.ds(0, 4)]),
                    (m_hbm.at[0], v.at[0]), (m_hbm.at[1], v.at[1]), (m_hbm.at[2], v.at[2]),
                    (temps_hbm, temps), (order_hbm, order), (accept_hbm, accept),
                    (j_hbm, jj),
                    (inv_d_hbm, inv_d), (inv_w_hbm, inv_w),
                    (masks_hbm.at[pl.ds(4, 4)], masks.at[pl.ds(4, 4)]),
                    (k_hbm, kk), (n_hbm, nn),
                )
            )
        ]
        first_loads, early_loads, late_loads = loads[:4], loads[4:10], loads[10:]
        barrier = pltpu.get_barrier_semaphore()
        for load in first_loads:
            load.start()

        def greet(step, carried):
            pl.semaphore_signal(
                barrier, inc=1, device_id=place(lax.rem(me + step, slices)), device_id_type=MESH
            )
            return carried

        lax.fori_loop(1, slices, greet, 0)
        for load in early_loads + late_loads:
            load.start()

        lane = lax.broadcasted_iota(jnp.int32, (width, depth), 1)
        next_one, last_one = (me + 1) % slices, (me + slices - 1) % slices

        def rows_of(index, pieces, piece):
            size = chunk // pieces
            return pl.ds(pl.multiple_of(index * chunk + piece * size, size), size)

        def exchange_copy(
            source, target, send_sem, recv_sem, pieces, component, piece, partner, origin
        ):
            return pltpu.make_async_remote_copy(
                src_ref=source.at[component, rows_of(partner, pieces, piece)],
                dst_ref=target.at[component, rows_of(origin, pieces, piece)],
                send_sem=send_sem.at[component, piece],
                recv_sem=recv_sem.at[component, piece],
                device_id=place(partner),
                device_id_type=MESH,
            )

        def own_copy(source, target, recv_sem, pieces, component, piece):
            return pltpu.make_async_copy(
                source.at[component, rows_of(me, pieces, piece)],
                target.at[component, rows_of(me, pieces, piece)],
                recv_sem.at[component, piece],
            )

        home = lax.div(me, layer)
        seat = lax.rem(me, layer)

        def send_layers(
            offsets, source, target, send_sem, recv_sem, pieces, component, piece
        ):
            for offset in offsets:
                away = home + offset

                @pl.when((away >= 0) & (away < layers))
                def _():
                    for turn_by in range(1 if offset == 0 else 0, layer):
                        partner = away * layer + lax.rem(seat + turn_by, layer)
                        exchange_copy(
                            source, target, send_sem, recv_sem, pieces, component, piece,
                            partner, me,
                        ).start()

        def send_near(source, target, send_sem, recv_sem, pieces, component, piece):
            send_layers((1, -1, 0), source, target, send_sem, recv_sem, pieces, component, piece)
            own_copy(source, target, recv_sem, pieces, component, piece).start()

        def bulk(source, target, send_sem, recv_sem, pieces, component, piece, count):
            rows_moved = pl.ds(0, count * (chunk // pieces))
            return pltpu.make_async_remote_copy(
                src_ref=source.at[component, rows_moved],
                dst_ref=target.at[component, rows_moved],
                send_sem=send_sem.at[component, piece],
                recv_sem=recv_sem.at[component, piece],
                device_id=place(last_one),
                device_id_type=MESH,
            )

        def receive_all(*route):
            bulk(*route, slices).wait_recv()

        def sent_all(*route):
            bulk(*route, slices - 1).wait_send()

        route_a = (send_a, recv_a, send_sem_a, recv_sem_a, 1)
        route_b = (send_b, recv_b, send_sem_b, recv_sem_b, parts)

        up_copy = pltpu.make_async_remote_copy(
            src_ref=carry, dst_ref=below, send_sem=halo_send.at[0], recv_sem=halo_recv.at[0],
            device_id=place(next_one), device_id_type=MESH,
        )
        down_copy = pltpu.make_async_remote_copy(
            src_ref=v.at[:, 0], dst_ref=above, send_sem=halo_send.at[1],
            recv_sem=halo_recv.at[1], device_id=place(last_one), device_id_type=MESH,
        )

        def widen():
            for r in range(rows):
                ky = me * rows + r
                high = jnp.where(ky > half, 1, 0)
                edge = jnp.where((ky == 0) | (ky == half), 1, 0)
                low_lane = jnp.where(lane < mid, 1, 0)
                flip0 = jnp.where(lane == 0, high, 0)
                flip1 = jnp.where(lane == mid, high, 0)
                edge0 = jnp.where(lane == 0, edge, 0)
                edge1 = jnp.where(lane == mid, edge, 0)
                take = (low_lane + flip0 + flip1 + edge1) % 2 == 1
                take_sine = (low_lane + flip0 + flip1 + edge0) % 2 == 1
                for item in range(6):
                    plain = kk[item, pl.ds(r, width, stride=rows), :]
                    other = turn(plain)
                    wide = jnp.where(take, plain, other)
                    kw[item, r] = wide
                    if r == 0:
                        ks[item] = jnp.where(take_sine, plain, other) - wide

        def forward_compute(component, start=0, stop=planes):
            for first in range(start, stop, per):
                group = range(first, first + per)
                packed = [dot_right(v[component, x], fwd_d[...]) for x in group]
                both = dot_left(fwd_w[...], jnp.concatenate(packed, axis=1))
                for number, x in enumerate(group):
                    part = slice(number * depth, (number + 1) * depth)
                    cosine, sine = both[:width, part], both[width:, part]
                    result = (
                        cosine * masks[0]
                        + turn(cosine) * masks[1]
                        + turn(sine) * masks[2]
                        + sine * masks[3]
                    )
                    for target in range(slices):
                        row = target * chunk + x * rows
                        send_a[component, row : row + rows, :] = result[
                            target * rows : (target + 1) * rows
                        ]

        def forward_component(component, carried):
            forward_compute(component)
            send_near(*route_a, component, 0)
            return carried

        def neighbours(step):
            def one(component, carried):
                for x in range(planes):
                    here = v[component, x]
                    ahead = above[component] if x == planes - 1 else v[component, x + 1]
                    total = jj[0, x].astype(F32) * ahead
                    if x == 0:
                        total = total + below[component]
                    else:
                        total = total + jj[0, x - 1].astype(F32) * v[component, x - 1]
                    bond = jj[1, x].astype(F32)
                    total = total + bond * pltpu.roll(here, width - 1, 0)
                    total = total + pltpu.roll(bond * here, 1, 0)
                    bond = jj[2, x].astype(F32)
                    total = total + bond * pltpu.roll(here, depth - 1, 1)
                    total = total + pltpu.roll(bond * here, 1, 1)
                    field[component, x] = total + scales[step, 0:1, :] * nn[step, component, x].astype(F32)
                return carried

            lax.fori_loop(0, 3, one, 0)

        def cross_forward(component, carried):
            receive_all(*route_a, component, 0)
            sign = jnp.where(lane < mid, 1.0, -1.0)
            for first in range(0, rows, per):
                group = range(first, first + per)
                lines = [recv_a[component, pl.ds(r, width, stride=rows), :] for r in group]
                both = dot_left(fwd_w[...], jnp.concatenate(lines, axis=1))
                for number, r in enumerate(group):
                    part = slice(number * depth, (number + 1) * depth)
                    cosine, sine = both[:width, part], both[width:, part]
                    sine = turn(sine) * sign
                    spec[component, r] = cosine + sine
                    if r == 0:
                        turned0[component] = sine
            return carried

        def cross_inverse(component):
            sign = jnp.where(lane < mid, -1.0, 1.0)
            items = PAIRS[component]
            for first in range(0, rows, per):
                group = range(first, first + per)
                plain, quarter = [], []
                for r in group:
                    value = (
                        kw[items[0], r] * spec[0, r]
                        + kw[items[1], r] * spec[1, r]
                        + kw[items[2], r] * spec[2, r]
                    )
                    if r == 0:
                        value = value + (
                            ks[items[0]] * turned0[0]
                            + ks[items[1]] * turned0[1]
                            + ks[items[2]] * turned0[2]
                        )
                    plain.append(value)
                    quarter.append(turn(value) * sign)
                stacked = jnp.concatenate(
                    [jnp.concatenate(plain, axis=1), jnp.concatenate(quarter, axis=1)], axis=0
                )
                result = dot_left(inv_w[...], stacked)
                for number, r in enumerate(group):
                    send_b[component, pl.ds(r, width, stride=rows), :] = result[
                        :, number * depth : (number + 1) * depth
                    ]
            for piece in range(parts):
                send_near(*route_b, component, piece)

        def inverse_component(piece, component, carried):
            receive_all(*route_b, component, piece)
            for first in range(piece * share, (piece + 1) * share, per):
                group = range(first, first + per)
                plain, quarter = [], []
                for x in group:
                    value = jnp.concatenate(
                        [
                            recv_b[component, s * chunk + x * rows : s * chunk + (x + 1) * rows, :]
                            for s in range(slices)
                        ],
                        axis=0,
                    )
                    other = turn(value)
                    plain.append(value * masks[4] + other * masks[5])
                    quarter.append(other * masks[6] + value * masks[7])
                stacked = jnp.concatenate(
                    [jnp.concatenate(plain, axis=1), jnp.concatenate(quarter, axis=1)], axis=0
                )
                result = dot_left(inv_w[...], stacked)
                for number, x in enumerate(group):
                    field[component, x] += dot_right(
                        result[:, number * depth : (number + 1) * depth], inv_d[...]
                    )
            return carried

        def advance(x, carried):
            block = math.gcd(width, 32)
            for start in range(0, width, block):
                part = slice(start, start + block)
                m = [v[c, x, part] for c in range(3)]
                h = [field[c, x, part] for c in range(3)]

                def product(a, b):
                    return [
                        a[1] * b[2] - a[2] * b[1],
                        a[2] * b[0] - a[0] * b[2],
                        a[0] * b[1] - a[1] * b[0],
                    ]

                t = product(m, h)
                w = product(m, t)
                u = [m[c] - TIME_STEP * (t[c] + DAMPING * w[c]) for c in range(3)]
                scale = lax.rsqrt(u[0] * u[0] + u[1] * u[1] + u[2] * u[2])
                for c in range(3):
                    moved = u[c] * scale
                    v[c, x, part] = moved
                    out[c, x, part] = moved
            return carried

        def relabel():
            count = temps.shape[0]
            replica = lax.axis_index("temp")

            def pick(source, index):
                chosen = source[0]
                for slot in range(1, count):
                    chosen = jnp.where(index == slot, source[slot], chosen)
                return chosen

            names = list(range(count))
            for pair in range(count // 2):
                first, second = order[2 * pair], order[2 * pair + 1]
                both = pick(accept, first) * pick(accept, second) == 1
                for slot in range(count):
                    names[slot] = jnp.where(
                        both & (first == slot),
                        second,
                        jnp.where(both & (second == slot), first, names[slot]),
                    )
            swapped = jnp.int32(0)
            for slot in range(count):
                labels[slot] = names[slot]
                swapped = jnp.where(replica == slot, names[slot], swapped)
            for step, index in enumerate((replica, swapped)):
                heat = jnp.full((8, depth), 2.0 * DAMPING / TIME_STEP * pick(temps, index), F32)
                scales[step] = jnp.sqrt(heat)

        for load in first_loads:
            load.wait()
        forward_compute(0)
        for load in early_loads:
            load.wait()
        relabel()
        pl.semaphore_wait(barrier, slices - 1)

        def step_body(step, carried):
            send_near(*route_a, 0, 0)
            for c in range(3):
                carry[c] = jj[0, planes - 1].astype(F32) * v[c, planes - 1]
            down_copy.start()
            up_copy.start()
            lax.fori_loop(1, 3, forward_component, 0)
            for c in range(3):
                send_layers((2, -2), *route_a, c, 0)
            for c in range(3):
                send_layers((3, -3), *route_a, c, 0)

            @pl.when(step == 0)
            def _():
                for load in late_loads:
                    load.wait()
                widen()

            up_copy.wait()
            down_copy.wait()
            neighbours(step)
            lax.fori_loop(0, 3, cross_forward, 0)
            for c in range(3):
                cross_inverse(c)
            for piece in range(parts):
                for c in range(3):
                    send_layers((2, -2), *route_b, c, piece)
                for c in range(3):
                    send_layers((3, -3), *route_b, c, piece)
            for c in range(3):
                sent_all(*route_a, c, 0)
            for piece in range(parts):
                lax.fori_loop(0, 3, functools.partial(inverse_component, piece), 0)
                lax.fori_loop(piece * share, (piece + 1) * share, advance, 0)

                @pl.when(step == 0)
                def _():
                    forward_compute(0, piece * share, (piece + 1) * share)

            for piece in range(parts):
                for c in range(3):
                    sent_all(*route_b, c, piece)
            return carried

        lax.fori_loop(0, 2, step_body, 0)

    return kernel


def on_device(moments, couplings, noise, kernel, temps, order, accept):
    planes, width, depth = moments.shape[2:]
    pens = lax.axis_size("pen")
    slices = lax.axis_size("slab") * pens
    rows = width // slices
    tables = [jnp.asarray(table) for table in build_tables(width, depth)]
    any_spec = pl.BlockSpec(memory_space=pl.ANY)
    cells = (3, planes, width, depth)
    flat = (3, width * rows, depth)
    dma = pltpu.SemaphoreType.DMA
    smem = pl.BlockSpec(memory_space=pltpu.SMEM)
    moved, labels = pl.pallas_call(
        make_kernel(slices, pens, planes, rows, width, depth),
        out_shape=(
            pltpu.VMEM(cells, F32),
            pltpu.SMEM(order.shape, jnp.int32),
        ),
        in_specs=[any_spec] * 12,
        out_specs=(pl.BlockSpec(memory_space=pltpu.VMEM), smem),
        scratch_shapes=[
            pltpu.SMEM(temps.shape, F32),
            pltpu.SMEM(order.shape, jnp.int32),
            pltpu.SMEM(accept.shape, jnp.int32),
            pltpu.VMEM((2, 8, depth), F32),
        ] + [pltpu.VMEM(table.shape, table.dtype) for table in tables] + [
            pltpu.VMEM(cells, F32),
            pltpu.VMEM(cells, BF16),
            pltpu.VMEM((2,) + cells, BF16),
            pltpu.VMEM((6, width * rows, depth), F32),
            pltpu.VMEM((6, rows, width, depth), F32),
            pltpu.VMEM((6, width, depth), F32),
            pltpu.VMEM((3, rows, width, depth), F32),
            pltpu.VMEM((3, width, depth), F32),
            pltpu.VMEM(cells, F32),
            pltpu.VMEM(flat, F32),
            pltpu.VMEM(flat, F32),
            pltpu.VMEM(flat, F32),
            pltpu.VMEM(flat, F32),
            pltpu.VMEM((3, width, depth), F32),
            pltpu.VMEM((3, width, depth), F32),
            pltpu.VMEM((3, width, depth), F32),
            dma((15,)),
            dma((3, 1)),
            dma((3, 1)),
            dma((3, 2)),
            dma((3, 2)),
            dma((2,)),
            dma((2,)),
        ],
        compiler_params=pltpu.CompilerParams(
            collective_id=0, has_side_effects=True, vmem_limit_bytes=60 * 1024 * 1024
        ),
        name="langevin",
    )(
        temps,
        order,
        accept,
        moments.reshape(cells),
        couplings,
        noise.reshape((2,) + cells),
        kernel.reshape(6, width * rows, depth),
        *tables,
    )
    return (moved.reshape(moments.shape), labels)


def solution(mesh):
    return jax.shard_map(
        on_device,
        mesh=mesh,
        in_specs=(
            P(("groups", "temp"), None, ("slab", "pen"), None, None),
            P("groups", ("slab", "pen"), None, None),
            P(None, ("groups", "temp"), None, ("slab", "pen"), None, None),
            P(None, None, ("slab", "pen"), None),
            P(),
            P("groups"),
            P("groups"),
        ),
        out_specs=(P(("groups", "temp"), None, ("slab", "pen"), None, None), P("groups")),
        check_vma=False,
    )
```

```python
import functools
import math

import jax
import jax.numpy as jnp
import numpy as np
from jax import lax
from jax.experimental import pallas as pl
from jax.experimental.pallas import tpu as pltpu
from jax.sharding import PartitionSpec as P

TIME_STEP = 0.1
DAMPING = 0.5
MESH = pl.DeviceIdType.MESH
F32 = jnp.float32
BF16 = jnp.bfloat16
PAIRS = ((0, 3, 4), (3, 1, 5), (4, 5, 2))


def trig(length):
    product = np.outer(np.arange(length), np.arange(length)) % length
    cosine = np.cos(2.0 * math.pi * product / length)
    sine = np.sin(2.0 * math.pi * product / length)
    sine[(2 * product) % length == 0] = 0.0
    return cosine, sine


def halves(table):
    table = table.astype(np.float32)
    high = table.astype(BF16)
    low = (table - high.astype(np.float32)).astype(BF16)
    return high, low


def left_table(table):
    high, low = halves(table)
    return np.concatenate([high, high, low], axis=1)


def right_table(table):
    high, low = halves(table)
    return np.concatenate([high, high, low], axis=0)


def split(values):
    high = values.astype(BF16)
    low = (values - high.astype(F32)).astype(BF16)
    return high, low


def dot_left(table, values):
    high, low = split(values)
    return jnp.dot(
        table, jnp.concatenate([high, low, high], axis=0), preferred_element_type=F32
    )


def dot_right(values, table):
    high, low = split(values)
    return jnp.dot(
        jnp.concatenate([high, low, high], axis=1), table, preferred_element_type=F32
    )


def build_tables(width, depth):
    cos_w, sin_w = trig(width)
    cos_d, sin_d = trig(depth)
    mid = depth // 2
    half = width // 2
    fwd_depth = np.concatenate([cos_d[:, :mid], -sin_d[:, :mid]], axis=1)
    fwd_depth[:, mid] = cos_d[:, mid]
    weight = np.where(np.arange(mid) == 0, 1.0, 2.0)[:, None]
    inv_depth = np.concatenate([weight * cos_d[:mid], -weight * sin_d[:mid]], axis=0)
    inv_depth[mid] = cos_d[mid]
    inv_depth = -inv_depth / depth
    fwd_width = np.concatenate([cos_w, sin_w], axis=0)
    inv_width = np.concatenate([cos_w, sin_w], axis=1) / width
    ky = np.arange(width)[:, None]
    lane = np.arange(depth)[None, :]
    lane0, lane_mid = lane == 0, lane == mid
    slot = lane0 | lane_mid
    low = (ky > 0) & (ky < half)
    high = ky > half
    edge = ~(low | high)
    sign = np.where(lane < mid, 1.0, -1.0)
    zero = np.zeros((width, depth))
    plain = zero + ~slot
    forward = [
        plain + (lane0 & ~high) + (lane_mid & edge),
        zero + (lane0 & high),
        plain * sign - (lane_mid & low),
        zero - (lane_mid & high),
    ]
    inverse = [
        plain + (slot & edge) + 2.0 * (lane0 & low),
        2.0 * (lane_mid & high),
        -plain * sign - 2.0 * (lane0 & low),
        -2.0 * (lane_mid & high),
    ]
    masks = np.stack(forward + inverse).astype(np.float32)
    return (
        right_table(fwd_depth),
        left_table(fwd_width),
        right_table(inv_depth),
        left_table(inv_width),
        masks,
    )


def make_kernel(slices, pens, planes, rows, width, depth):
    mid = depth // 2
    half = width // 2
    chunk = planes * rows
    per = 4
    parts = 2 if planes % (2 * per) == 0 and planes * rows % 16 == 0 else 1
    share = planes // parts
    layer = max(1, slices // 4)
    layers = slices // layer

    def turn(values):
        return pltpu.roll(values, mid, 1)

    def kernel(
        temps_hbm, order_hbm, accept_hbm, m_hbm, j_hbm, n_hbm, k_hbm,
        fwd_d_hbm, fwd_w_hbm, inv_d_hbm, inv_w_hbm, masks_hbm,
        out, labels, temps, order, accept, scales, fwd_d, fwd_w, inv_d, inv_w, masks,
        v, jj, nn, kk, kw, ks, spec, turned0, field, send_a, recv_a, send_b, recv_b,
        carry, above, below,
        load_sem, send_sem_a, recv_sem_a, send_sem_b, recv_sem_b, halo_send, halo_recv,
    ):
        me = lax.axis_index("slab") * pens + lax.axis_index("pen")

        def place(index):
            return {"slab": lax.div(index, pens), "pen": lax.rem(index, pens)}

        loads = [
            pltpu.make_async_copy(source, target, load_sem.at[number])
            for number, (source, target) in enumerate(
                (
                    (fwd_d_hbm, fwd_d), (fwd_w_hbm, fwd_w),
                    (masks_hbm.at[pl.ds(0, 4)], masks.at[pl.ds(0, 4)]),
                    (m_hbm.at[0], v.at[0]), (m_hbm.at[1], v.at[1]), (m_hbm.at[2], v.at[2]),
                    (temps_hbm, temps), (order_hbm, order), (accept_hbm, accept),
                    (j_hbm, jj),
                    (inv_d_hbm, inv_d), (inv_w_hbm, inv_w),
                    (masks_hbm.at[pl.ds(4, 4)], masks.at[pl.ds(4, 4)]),
                    (k_hbm, kk), (n_hbm, nn),
                )
            )
        ]
        first_loads, early_loads, late_loads = loads[:4], loads[4:10], loads[10:]
        barrier = pltpu.get_barrier_semaphore()
        for load in first_loads:
            load.start()

        def greet(step, carried):
            pl.semaphore_signal(
                barrier, inc=1, device_id=place(lax.rem(me + step, slices)), device_id_type=MESH
            )
            return carried

        lax.fori_loop(1, slices, greet, 0)
        for load in early_loads + late_loads:
            load.start()

        lane = lax.broadcasted_iota(jnp.int32, (width, depth), 1)
        next_one, last_one = (me + 1) % slices, (me + slices - 1) % slices

        def rows_of(index, pieces, piece):
            size = chunk // pieces
            return pl.ds(pl.multiple_of(index * chunk + piece * size, size), size)

        def exchange_copy(
            source, target, send_sem, recv_sem, pieces, component, piece, partner, origin
        ):
            return pltpu.make_async_remote_copy(
                src_ref=source.at[component, rows_of(partner, pieces, piece)],
                dst_ref=target.at[component, rows_of(origin, pieces, piece)],
                send_sem=send_sem.at[component, piece],
                recv_sem=recv_sem.at[component, piece],
                device_id=place(partner),
                device_id_type=MESH,
            )

        def own_copy(source, target, recv_sem, pieces, component, piece):
            return pltpu.make_async_copy(
                source.at[component, rows_of(me, pieces, piece)],
                target.at[component, rows_of(me, pieces, piece)],
                recv_sem.at[component, piece],
            )

        home = lax.div(me, layer)
        seat = lax.rem(me, layer)

        def send_layers(
            offsets, source, target, send_sem, recv_sem, pieces, component, piece
        ):
            for offset in offsets:
                away = home + offset

                @pl.when((away >= 0) & (away < layers))
                def _():
                    for turn_by in range(1 if offset == 0 else 0, layer):
                        partner = away * layer + lax.rem(seat + turn_by, layer)
                        exchange_copy(
                            source, target, send_sem, recv_sem, pieces, component, piece,
                            partner, me,
                        ).start()

        def send_near(source, target, send_sem, recv_sem, pieces, component, piece):
            send_layers((1, -1, 0), source, target, send_sem, recv_sem, pieces, component, piece)
            own_copy(source, target, recv_sem, pieces, component, piece).start()

        def bulk(source, target, send_sem, recv_sem, pieces, component, piece, count):
            rows_moved = pl.ds(0, count * (chunk // pieces))
            return pltpu.make_async_remote_copy(
                src_ref=source.at[component, rows_moved],
                dst_ref=target.at[component, rows_moved],
                send_sem=send_sem.at[component, piece],
                recv_sem=recv_sem.at[component, piece],
                device_id=place(last_one),
                device_id_type=MESH,
            )

        def receive_all(*route):
            bulk(*route, slices).wait_recv()

        def sent_all(*route):
            bulk(*route, slices - 1).wait_send()

        route_a = (send_a, recv_a, send_sem_a, recv_sem_a, 1)
        route_b = (send_b, recv_b, send_sem_b, recv_sem_b, parts)

        up_copy = pltpu.make_async_remote_copy(
            src_ref=carry, dst_ref=below, send_sem=halo_send.at[0], recv_sem=halo_recv.at[0],
            device_id=place(next_one), device_id_type=MESH,
        )
        down_copy = pltpu.make_async_remote_copy(
            src_ref=v.at[:, 0], dst_ref=above, send_sem=halo_send.at[1],
            recv_sem=halo_recv.at[1], device_id=place(last_one), device_id_type=MESH,
        )

        def widen():
            for r in range(rows):
                ky = me * rows + r
                high = jnp.where(ky > half, 1, 0)
                edge = jnp.where((ky == 0) | (ky == half), 1, 0)
                low_lane = jnp.where(lane < mid, 1, 0)
                flip0 = jnp.where(lane == 0, high, 0)
                flip1 = jnp.where(lane == mid, high, 0)
                edge0 = jnp.where(lane == 0, edge, 0)
                edge1 = jnp.where(lane == mid, edge, 0)
                take = (low_lane + flip0 + flip1 + edge1) % 2 == 1
                take_sine = (low_lane + flip0 + flip1 + edge0) % 2 == 1
                for item in range(6):
                    plain = kk[item, pl.ds(r, width, stride=rows), :]
                    other = turn(plain)
                    wide = jnp.where(take, plain, other)
                    kw[item, r] = wide
                    if r == 0:
                        ks[item] = jnp.where(take_sine, plain, other) - wide

        def forward_compute(component, start=0, stop=planes):
            for first in range(start, stop, per):
                group = range(first, first + per)
                packed = [dot_right(v[component, x], fwd_d[...]) for x in group]
                both = dot_left(fwd_w[...], jnp.concatenate(packed, axis=1))
                for number, x in enumerate(group):
                    part = slice(number * depth, (number + 1) * depth)
                    cosine, sine = both[:width, part], both[width:, part]
                    result = (
                        cosine * masks[0]
                        + turn(cosine) * masks[1]
                        + turn(sine) * masks[2]
                        + sine * masks[3]
                    )
                    for target in range(slices):
                        row = target * chunk + x * rows
                        send_a[component, row : row + rows, :] = result[
                            target * rows : (target + 1) * rows
                        ]

        def forward_component(component, carried):
            forward_compute(component)
            send_near(*route_a, component, 0)
            return carried

        def neighbours(step):
            def one(component, carried):
                for x in range(planes):
                    here = v[component, x]
                    ahead = above[component] if x == planes - 1 else v[component, x + 1]
                    total = jj[0, x].astype(F32) * ahead
                    if x == 0:
                        total = total + below[component]
                    else:
                        total = total + jj[0, x - 1].astype(F32) * v[component, x - 1]
                    bond = jj[1, x].astype(F32)
                    total = total + bond * pltpu.roll(here, width - 1, 0)
                    total = total + pltpu.roll(bond * here, 1, 0)
                    bond = jj[2, x].astype(F32)
                    total = total + bond * pltpu.roll(here, depth - 1, 1)
                    total = total + pltpu.roll(bond * here, 1, 1)
                    field[component, x] = total + scales[step, 0:1, :] * nn[step, component, x].astype(F32)
                return carried

            lax.fori_loop(0, 3, one, 0)

        def cross_forward(component, carried):
            receive_all(*route_a, component, 0)
            sign = jnp.where(lane < mid, 1.0, -1.0)
            for first in range(0, rows, per):
                group = range(first, first + per)
                lines = [recv_a[component, pl.ds(r, width, stride=rows), :] for r in group]
                both = dot_left(fwd_w[...], jnp.concatenate(lines, axis=1))
                for number, r in enumerate(group):
                    part = slice(number * depth, (number + 1) * depth)
                    cosine, sine = both[:width, part], both[width:, part]
                    sine = turn(sine) * sign
                    spec[component, r] = cosine + sine
                    if r == 0:
                        turned0[component] = sine
            return carried

        def cross_inverse(component):
            sign = jnp.where(lane < mid, -1.0, 1.0)
            items = PAIRS[component]
            for first in range(0, rows, per):
                group = range(first, first + per)
                plain, quarter = [], []
                for r in group:
                    value = (
                        kw[items[0], r] * spec[0, r]
                        + kw[items[1], r] * spec[1, r]
                        + kw[items[2], r] * spec[2, r]
                    )
                    if r == 0:
                        value = value + (
                            ks[items[0]] * turned0[0]
                            + ks[items[1]] * turned0[1]
                            + ks[items[2]] * turned0[2]
                        )
                    plain.append(value)
                    quarter.append(turn(value) * sign)
                stacked = jnp.concatenate(
                    [jnp.concatenate(plain, axis=1), jnp.concatenate(quarter, axis=1)], axis=0
                )
                result = dot_left(inv_w[...], stacked)
                for number, r in enumerate(group):
                    send_b[component, pl.ds(r, width, stride=rows), :] = result[
                        :, number * depth : (number + 1) * depth
                    ]
            for piece in range(parts):
                send_near(*route_b, component, piece)

        def inverse_component(piece, component, carried):
            receive_all(*route_b, component, piece)
            for first in range(piece * share, (piece + 1) * share, per):
                group = range(first, first + per)
                plain, quarter = [], []
                for x in group:
                    value = jnp.concatenate(
                        [
                            recv_b[component, s * chunk + x * rows : s * chunk + (x + 1) * rows, :]
                            for s in range(slices)
                        ],
                        axis=0,
                    )
                    other = turn(value)
                    plain.append(value * masks[4] + other * masks[5])
                    quarter.append(other * masks[6] + value * masks[7])
                stacked = jnp.concatenate(
                    [jnp.concatenate(plain, axis=1), jnp.concatenate(quarter, axis=1)], axis=0
                )
                result = dot_left(inv_w[...], stacked)
                for number, x in enumerate(group):
                    field[component, x] += dot_right(
                        result[:, number * depth : (number + 1) * depth], inv_d[...]
                    )
            return carried

        def advance(x, carried):
            block = math.gcd(width, 32)
            for start in range(0, width, block):
                part = slice(start, start + block)
                m = [v[c, x, part] for c in range(3)]
                h = [field[c, x, part] for c in range(3)]

                def product(a, b):
                    return [
                        a[1] * b[2] - a[2] * b[1],
                        a[2] * b[0] - a[0] * b[2],
                        a[0] * b[1] - a[1] * b[0],
                    ]

                t = product(m, h)
                w = product(m, t)
                u = [m[c] - TIME_STEP * (t[c] + DAMPING * w[c]) for c in range(3)]
                scale = lax.rsqrt(u[0] * u[0] + u[1] * u[1] + u[2] * u[2])
                for c in range(3):
                    moved = u[c] * scale
                    v[c, x, part] = moved
                    out[c, x, part] = moved
            return carried

        def relabel():
            count = temps.shape[0]
            replica = lax.axis_index("temp")

            def pick(source, index):
                chosen = source[0]
                for slot in range(1, count):
                    chosen = jnp.where(index == slot, source[slot], chosen)
                return chosen

            names = list(range(count))
            for pair in range(count // 2):
                first, second = order[2 * pair], order[2 * pair + 1]
                both = pick(accept, first) * pick(accept, second) == 1
                for slot in range(count):
                    names[slot] = jnp.where(
                        both & (first == slot),
                        second,
                        jnp.where(both & (second == slot), first, names[slot]),
                    )
            swapped = jnp.int32(0)
            for slot in range(count):
                labels[slot] = names[slot]
                swapped = jnp.where(replica == slot, names[slot], swapped)
            for step, index in enumerate((replica, swapped)):
                heat = jnp.full((8, depth), 2.0 * DAMPING / TIME_STEP * pick(temps, index), F32)
                scales[step] = jnp.sqrt(heat)

        for load in first_loads:
            load.wait()
        forward_compute(0)
        for load in early_loads:
            load.wait()
        relabel()
        pl.semaphore_wait(barrier, slices - 1)

        def step_body(step, carried):
            send_near(*route_a, 0, 0)
            for c in range(3):
                carry[c] = jj[0, planes - 1].astype(F32) * v[c, planes - 1]
            down_copy.start()
            up_copy.start()
            lax.fori_loop(1, 3, forward_component, 0)
            for c in range(3):
                send_layers((2, -2), *route_a, c, 0)
            for c in range(3):
                send_layers((3, -3), *route_a, c, 0)

            @pl.when(step == 0)
            def _():
                for load in late_loads:
                    load.wait()
                widen()

            up_copy.wait()
            down_copy.wait()
            neighbours(step)
            lax.fori_loop(0, 3, cross_forward, 0)
            for c in range(3):
                cross_inverse(c)
            for piece in range(parts):
                for c in range(3):
                    send_layers((2, -2), *route_b, c, piece)
                for c in range(3):
                    send_layers((3, -3), *route_b, c, piece)
            for c in range(3):
                sent_all(*route_a, c, 0)
            for piece in range(parts):
                lax.fori_loop(0, 3, functools.partial(inverse_component, piece), 0)
                lax.fori_loop(piece * share, (piece + 1) * share, advance, 0)

                @pl.when(step == 0)
                def _():
                    forward_compute(0, piece * share, (piece + 1) * share)

            for piece in range(parts):
                for c in range(3):
                    sent_all(*route_b, c, piece)
            return carried

        lax.fori_loop(0, 2, step_body, 0)

    return kernel


def on_device(moments, couplings, noise, kernel, temps, order, accept):
    planes, width, depth = moments.shape[2:]
    pens = lax.axis_size("pen")
    slices = lax.axis_size("slab") * pens
    rows = width // slices
    tables = [jnp.asarray(table) for table in build_tables(width, depth)]
    any_spec = pl.BlockSpec(memory_space=pl.ANY)
    cells = (3, planes, width, depth)
    flat = (3, width * rows, depth)
    dma = pltpu.SemaphoreType.DMA
    smem = pl.BlockSpec(memory_space=pltpu.SMEM)
    moved, labels = pl.pallas_call(
        make_kernel(slices, pens, planes, rows, width, depth),
        out_shape=(
            pltpu.VMEM(cells, F32),
            pltpu.SMEM(order.shape, jnp.int32),
        ),
        in_specs=[any_spec] * 12,
        out_specs=(pl.BlockSpec(memory_space=pltpu.VMEM), smem),
        scratch_shapes=[
            pltpu.SMEM(temps.shape, F32),
            pltpu.SMEM(order.shape, jnp.int32),
            pltpu.SMEM(accept.shape, jnp.int32),
            pltpu.VMEM((2, 8, depth), F32),
        ] + [pltpu.VMEM(table.shape, table.dtype) for table in tables] + [
            pltpu.VMEM(cells, F32),
            pltpu.VMEM(cells, BF16),
            pltpu.VMEM((2,) + cells, BF16),
            pltpu.VMEM((6, width * rows, depth), F32),
            pltpu.VMEM((6, rows, width, depth), F32),
            pltpu.VMEM((6, width, depth), F32),
            pltpu.VMEM((3, rows, width, depth), F32),
            pltpu.VMEM((3, width, depth), F32),
            pltpu.VMEM(cells, F32),
            pltpu.VMEM(flat, F32),
            pltpu.VMEM(flat, F32),
            pltpu.VMEM(flat, F32),
            pltpu.VMEM(flat, F32),
            pltpu.VMEM((3, width, depth), F32),
            pltpu.VMEM((3, width, depth), F32),
            pltpu.VMEM((3, width, depth), F32),
            dma((15,)),
            dma((3, 1)),
            dma((3, 1)),
            dma((3, 2)),
            dma((3, 2)),
            dma((2,)),
            dma((2,)),
        ],
        compiler_params=pltpu.CompilerParams(
            collective_id=0, has_side_effects=True, vmem_limit_bytes=60 * 1024 * 1024
        ),
        name="langevin",
    )(
        temps,
        order,
        accept,
        moments.reshape(cells),
        couplings,
        noise.reshape((2,) + cells),
        kernel.reshape(6, width * rows, depth),
        *tables,
    )
    return (moved.reshape(moments.shape), labels)


def solution(mesh):
    return jax.shard_map(
        on_device,
        mesh=mesh,
        in_specs=(
            P(("groups", "temp"), None, ("slab", "pen"), None, None),
            P("groups", ("slab", "pen"), None, None),
            P(None, ("groups", "temp"), None, ("slab", "pen"), None, None),
            P(None, None, ("slab", "pen"), None),
            P(),
            P("groups"),
            P("groups"),
        ),
        out_specs=(P(("groups", "temp"), None, ("slab", "pen"), None, None), P("groups")),
        check_vma=False,
    )
```
